32 devices in a mesh: fsdp: 8 (over z, x), tile: 4 (over y, core).
Axes of the slice: x: 2, y: 2, z: 4, core: 2. Of those that a mesh axis runs over, the one named last changes fastest.
Arguments:
- tokens: bfloat16 [8192, 1536], P('fsdp', 'tile'), may hold values from -6 to 6
- ln_gain: float32 [1536], replicated, may hold values from 0.25 to 1.75
- w_up: bfloat16 [1536, 6144], P('fsdp', 'tile'), may hold values from -0.15625 to 0.15625
- w_down: bfloat16 [6144, 1536], P('tile', 'fsdp'), may hold values from -0.078125 to 0.078125
- w_flux_in: bfloat16 [1536, 768], P('tile'), may hold values from -0.15625 to 0.15625
- w_flux_out: bfloat16 [768, 128], replicated, may hold values from -0.21875 to 0.21875
- ocean_state: bfloat16 [256, 128, 256], P('fsdp', 'tile'), may hold values from -6 to 6
- land_mask: int32 [256, 128], P('fsdp', 'tile'), may hold values from 0 to 1, as said below
- column_map: int32 [256, 128], P('fsdp', 'tile'), may hold values from 0 to 8191, as said below
- w_couple: bfloat16 [128, 256], replicated, may hold values from -0.5 to 0.5
- dw_kernel: float32 [2, 7, 7, 256], replicated, may hold values from -0.875 to 0.875
- ocean_gain: float32 [2, 256], replicated, may hold values from 0.25 to 1.75
- w_pw1: bfloat16 [2, 256, 1024], replicated, may hold values from -0.375 to 0.375
- w_pw2: bfloat16 [2, 1024, 256], replicated, may hold values from -0.1875 to 0.1875
Outputs:
- atm_out: bfloat16 [8192, 1536], P('fsdp', 'tile')
- ocean_out: bfloat16 [256, 128, 256], P('fsdp', 'tile')
The draws below stay inside these ranges and needn't reach their ends.
Inputs may be any that keep to these rules, and one draw needn't show every extreme that they name: `land_mask`: 0 or 1; land comes in regions of 8 x 8 cells whose ocean share varies. `column_map`: the column in grid row x names a token between (x // 32) * 1024 - 256 and (x // 32 + 1) * 1024 + 255.
All inputs are finite; a program needn't handle non-finite values.
Results may differ from the reference program's by a relative error of at most 0.014.
Values may be sent and summed in bfloat16 or wider, within the bound.
No kernel may reach another device: no remote copies, remote signals or barrier semaphores. Data moves between devices by JAX's collectives and lax.ppermute only.
A program may use at most 128 MiB of HBM per device.

```python
import jax
import jax.numpy as jnp
from jax import lax

D = 1536
FF = 6144
FH = 768
FLX = 128
OC = 256
OH = 1024
KS = 7
BLOCKS = 2
TOK_DEV = 1024
OX = 32
RIM = 256
TOKENS = 8192
NOX = 256
NOY = 128
N_FSDP = 8


def draw_land_mask(key, part):
    first, second = jax.random.split(jax.random.fold_in(key, 11))
    patch_rows = NOX // 8 + 1
    patch_cols = NOY // 8 + 1
    levels = jax.random.randint(first, (patch_rows, patch_cols), 2, 11)
    levels = jnp.repeat(jnp.repeat(levels, 8, axis=0), 8, axis=1)[:NOX, :NOY]
    cells = jax.random.randint(second, (NOX, NOY), 0, 10)
    return (cells < levels).astype(jnp.int32)


def draw_column_map(key, part):
    offsets = jax.random.randint(jax.random.fold_in(key, 23), (NOX, NOY), 0, TOK_DEV + 2 * RIM)
    band = jnp.arange(NOX, dtype=jnp.int32) // OX
    start = band * TOK_DEV - RIM
    return jnp.clip(start[:, None] + offsets, 0, TOKENS - 1).astype(jnp.int32)


def shard_levels(stream_key, extent, cuts, low, top_value):
    def one(axis_at, blocks):
        draws = jax.random.uniform(jax.random.fold_in(jax.random.fold_in(stream_key, 6), axis_at), (blocks,), jnp.float32, low / len(cuts), top_value / len(cuts))
        return jnp.repeat(jnp.exp(draws), extent[axis_at] // blocks).reshape((-1,) + (1,) * (len(extent) - axis_at - 1))

    level = one(*cuts[0])
    for cut in cuts[1:]:
        level = level * one(*cut)
    return level


def gaussian(stream_key, dims, scale, reach, shards=(), kind=jnp.bfloat16):
    level = shard_levels(stream_key, dims, shards, -0.22, 0.18) if shards else 1.0
    result = jax.random.normal(stream_key, dims, jnp.float32) * scale * level
    return jnp.minimum(jnp.maximum(result, -reach), reach).astype(kind)


def setup_inputs(seed: int = 0) -> dict:
    seeds = jax.random.split(jax.random.key(seed), 15)
    return {
        "tokens": gaussian(seeds[0], (TOKENS, D), 1.0, 6.0, ((0, 8), (1, 4))),
        "ln_gain": jnp.clip(1.0 + 0.15 * jax.random.normal(seeds[1], (D,), jnp.float32), 0.25, 1.75),
        "w_up": gaussian(seeds[2], (D, FF), D ** -0.5, 0.15625, ((0, 8), (1, 4))),
        "w_down": gaussian(seeds[3], (FF, D), FF ** -0.5, 0.078125, ((0, 4), (1, 8))),
        "w_flux_in": gaussian(seeds[4], (D, FH), D ** -0.5, 0.15625, ((0, 4),)),
        "w_flux_out": gaussian(seeds[5], (FH, FLX), FH ** -0.5, 0.21875),
        "ocean_state": gaussian(seeds[6], (NOX, NOY, OC), 1.0, 6.0, ((0, 8), (1, 4))),
        "land_mask": draw_land_mask(jax.random.fold_in(seeds[14], 71), 0),
        "column_map": draw_column_map(jax.random.fold_in(seeds[14], 71), 0),
        "w_couple": gaussian(seeds[9], (FLX, OC), FLX ** -0.5, 0.5),
        "dw_kernel": gaussian(seeds[10], (BLOCKS, KS, KS, OC), (KS * KS) ** -0.5, 0.875, (), jnp.float32),
        "ocean_gain": jnp.clip(1.0 + 0.15 * jax.random.normal(seeds[11], (BLOCKS, OC), jnp.float32), 0.25, 1.75),
        "w_pw1": gaussian(seeds[12], (BLOCKS, OC, OH), OC ** -0.5, 0.375),
        "w_pw2": gaussian(seeds[13], (BLOCKS, OH, OC), OH ** -0.5, 0.1875),
    }


def layer_norm(values, gain):
    center = values - lax.optimization_barrier(jnp.mean(values, axis=-1, keepdims=True))
    spread = lax.optimization_barrier(jnp.mean(center * center, axis=-1, keepdims=True))
    return center * lax.rsqrt(spread + 1e-06) * gain

def conv_block(padded, region_mask, kernel, gain, w_one, w_two):
    rows = padded.shape[0] - 6
    cols = padded.shape[1] - 6
    chans = padded.shape[2]
    total = jnp.zeros((rows, cols, chans), jnp.float32)
    for first in range(7):
        for second in range(7):
            total = total + padded[first:first + rows, second:second + cols].astype(jnp.float32) * kernel[first, second]
    pnorm = layer_norm(total, gain).astype(jnp.bfloat16).reshape(rows * cols, chans)
    inner = jax.nn.gelu(jnp.dot(pnorm, w_one, preferred_element_type=jnp.float32), approximate=True).astype(jnp.bfloat16)
    lowered = jnp.dot(inner, w_two, preferred_element_type=jnp.float32).reshape(rows, cols, chans)
    before = padded[3:3 + rows, 3:3 + cols].astype(jnp.float32)
    return (region_mask[..., None] * (before + lowered)).astype(jnp.bfloat16)

def reference(tokens, ln_gain, w_up, w_down, w_flux_in, w_flux_out, ocean_state, land_mask, column_map, w_couple, dw_kernel, ocean_gain, w_pw1, w_pw2):
    bands = tokens.reshape(N_FSDP, TOK_DEV, D)

    def one_band(band):
        normed = layer_norm(band.astype(jnp.float32), ln_gain).astype(jnp.bfloat16)
        hidden = jax.nn.gelu(jnp.dot(normed, w_up, preferred_element_type=jnp.float32), approximate=True).astype(jnp.bfloat16)
        atm_band = (band.astype(jnp.float32) + jnp.dot(hidden, w_down, preferred_element_type=jnp.float32)).astype(jnp.bfloat16)
        flux_hidden = jax.nn.gelu(jnp.dot(atm_band, w_flux_in, preferred_element_type=jnp.float32), approximate=True).astype(jnp.bfloat16)
        fluxes = jnp.dot(flux_hidden, w_flux_out, preferred_element_type=jnp.float32).astype(jnp.bfloat16)
        return (atm_band, fluxes)
    atm_bands, flux_bands = lax.map(one_band, bands)
    atm_out = atm_bands.reshape(TOKENS, D)
    fluxes = flux_bands.reshape(TOKENS, FLX)
    mask = land_mask.astype(jnp.float32)
    picked = jnp.take(fluxes, column_map.reshape(-1).astype(jnp.int32), axis=0)
    forcing = jnp.dot(picked, w_couple, preferred_element_type=jnp.float32).reshape(NOX, NOY, OC)
    state = (mask[..., None] * (ocean_state.astype(jnp.float32) + forcing)).astype(jnp.bfloat16)
    for block in range(BLOCKS):
        padded = jnp.pad(state, ((3, 3), (3, 3), (0, 0)))
        state = conv_block(padded, mask, dw_kernel[block], ocean_gain[block], w_pw1[block], w_pw2[block])
    return (atm_out, state)
```

```python
import functools

import jax
import jax.numpy as jnp
from jax import lax
from jax.experimental import pallas as pl
from jax.experimental.pallas import tpu as pltpu
from jax.sharding import PartitionSpec as P

EPS = 1e-06
BF = jnp.bfloat16
F32 = jnp.float32


def move(value, axis, target):
    count = lax.axis_size(axis)
    pairs = [(i, target(i)) for i in range(count)]
    return lax.ppermute(value, axis, [(i, j) for i, j in pairs if 0 <= j < count])


def across_x(value):
    return move(value, "fsdp", lambda i: i ^ 1)


def across_y(value):
    return move(value, "tile", lambda i: i ^ 2)


def across_core(value):
    return move(value, "tile", lambda i: i ^ 1)


def across_both(value):
    return move(value, "tile", lambda i: i ^ 3)


def line_move(value, pairs):
    both = [(2 * a + x, 2 * b + x) for a, b in pairs for x in range(2)]
    return lax.ppermute(value, "fsdp", both)


def line_gather(value, layer):
    layers = lax.axis_size("fsdp") // 2
    if layers == 4:
        far = line_move(value, [(0, 2), (2, 0), (1, 3), (3, 1)])
        near = line_move(value, [(0, 1), (1, 0), (2, 3), (3, 2)])
        middle = line_move(value, [(1, 2), (2, 1)])
        outer = line_move(far, [(2, 3), (1, 0)])
        inner = (layer == 1) | (layer == 2)
        return [value, near, far, jnp.where(inner, middle, outer)]
    blocks = value[None]
    step = 1
    while step < layers:
        pairs = [(i, i ^ step) for i in range(layers)]
        blocks = jnp.concatenate([blocks, line_move(blocks, pairs)], axis=0)
        step *= 2
    return [blocks[i] for i in range(layers)]


def in_order(first, own, other, axis):
    return jnp.where(
        first,
        jnp.concatenate([own, other], axis=axis),
        jnp.concatenate([other, own], axis=axis),
    )


def norm_kernel(order, p0, p1, p2, p3, gain_ref, normed_ref, raw_ref):
    step = pl.program_id(0)
    pieces = [p0, p1, p2, p3]
    width = p0.shape[-1]
    values = [p[0].astype(F32) for p in pieces]
    whole = width * len(pieces)
    mean = sum(jnp.sum(v, axis=-1, keepdims=True) for v in values) / whole
    centers = [v - mean for v in values]
    spread = sum(jnp.sum(c * c, axis=-1, keepdims=True) for c in centers) / whole
    scale = lax.rsqrt(spread + EPS)
    for i, center in enumerate(centers):
        start = pl.multiple_of(order[8 + i] * width, width)
        gain = gain_ref[:, pl.ds(start, width)]
        normed_ref[:, pl.ds(start, width)] = (center * scale * gain).astype(BF)

    @pl.when(step == 0)
    def _():
        for i, p in enumerate(pieces):
            start = pl.multiple_of(order[8 + i] * width, width)
            raw_ref[:, pl.ds(start, width)] = p[0]


def normalise(pieces, order, gain):
    blocks, rows, width = pieces[0].shape
    whole = width * len(pieces)
    spec = pl.BlockSpec((1, rows, width), lambda i, o: (o[i], 0, 0))
    return pl.pallas_call(
        norm_kernel,
        out_shape=(
            jax.ShapeDtypeStruct((blocks * rows, whole), BF),
            jax.ShapeDtypeStruct((rows, whole), BF),
        ),
        grid_spec=pltpu.PrefetchScalarGridSpec(
            num_scalar_prefetch=1,
            grid=(blocks,),
            in_specs=[spec] * 4 + [pl.BlockSpec((1, whole), lambda i, o: (0, 0))],
            out_specs=(
                pl.BlockSpec((rows, whole), lambda i, o: (i, 0)),
                pl.BlockSpec((rows, whole), lambda i, o: (0, 0)),
            ),
        ),
        name="normalise",
    )(order, *pieces, gain.reshape(1, whole))


def layer_norm(values, gain):
    center = values - jnp.mean(values, axis=-1, keepdims=True)
    spread = jnp.mean(center * center, axis=-1, keepdims=True)
    return center * lax.rsqrt(spread + EPS) * gain


def conv_block(padded, region_mask, kernel, gain, w_one, w_two):
    rows = padded.shape[0] - 6
    cols = padded.shape[1] - 6
    chans = padded.shape[2]
    total = jnp.zeros((rows, cols, chans), F32)
    for first in range(7):
        for second in range(7):
            total = (
                total
                + padded[first : first + rows, second : second + cols].astype(F32)
                * kernel[first, second]
            )
    pnorm = layer_norm(total, gain).astype(BF).reshape(rows * cols, chans)
    inner = jax.nn.gelu(
        jnp.dot(pnorm, w_one, preferred_element_type=F32), approximate=True
    ).astype(BF)
    lowered = jnp.dot(inner, w_two, preferred_element_type=F32).reshape(rows, cols, chans)
    before = padded[3 : 3 + rows, 3 : 3 + cols].astype(F32)
    return (region_mask[..., None] * (before + lowered)).astype(BF)


def side_halo(block, axis, dim, width):
    low = move(lax.slice_in_dim(block, block.shape[dim] - width, None, axis=dim), axis, lambda i: i + 1)
    high = move(lax.slice_in_dim(block, 0, width, axis=dim), axis, lambda i: i - 1)
    return jnp.concatenate([low, block, high], axis=dim)


def body(
    tokens,
    ln_gain,
    w_up,
    w_down,
    w_flux_in,
    w_flux_out,
    ocean_state,
    land_mask,
    column_map,
    w_couple,
    dw_kernel,
    ocean_gain,
    w_pw1,
    w_pw2,
):
    band = lax.axis_index("fsdp")
    tile = lax.axis_index("tile")
    side = band % 2
    layer = band // 2
    first = side == 0
    layers = lax.axis_size("fsdp") // 2
    band_rows, token_cols = tokens.shape
    depth, hidden_cols = w_up.shape
    half = hidden_cols // 2
    quarter = band_rows // 4
    width = token_cols * 4
    block_cols = 2 * depth

    up_own = lax.dynamic_slice(w_up, (0, side * half), (depth, half))
    up_away = lax.dynamic_slice(w_up, (0, (1 - side) * half), (depth, half))
    down_own = lax.dynamic_slice(w_down, (side * half, 0), (half, depth))
    down_away = lax.dynamic_slice(w_down, ((1 - side) * half, 0), (half, depth))

    up_other = across_x(up_away)
    up_own_blocks = line_gather(up_own, layer)
    up_other_blocks = line_gather(up_other, layer)

    tok_x = across_x(tokens)
    tok_y = across_y(tokens)
    tok_xy = across_y(tok_x)
    tok_c = across_core(jnp.stack([tokens, tok_x]))
    tok_yc = across_core(jnp.stack([tok_y, tok_xy]))

    down_other = across_x(down_away)
    down_block = in_order(first, down_own, down_other, 1)
    down_blocks = line_gather(down_block, layer)

    flux_y = across_y(w_flux_in)
    flux_c = across_core(jnp.stack([w_flux_in, flux_y]))
    flux_in = jnp.zeros((width, w_flux_in.shape[1]), BF)
    for i, piece in enumerate([w_flux_in, flux_c[0], flux_y, flux_c[1]]):
        flux_in = lax.dynamic_update_slice(flux_in, piece, ((tile ^ i) * token_cols, 0))

    halo = 6
    packed = column_map * 2 + land_mask
    packed = side_halo(packed, "tile", 1, halo)
    wide_state = side_halo(ocean_state, "tile", 1, halo)
    wide_mask = packed & 1
    wide_map = packed >> 1
    full_mask = side_halo(wide_mask, "fsdp", 0, halo)

    def rows_of(own, other):
        return jnp.concatenate(
            [own.reshape(4, quarter, token_cols), other.reshape(4, quarter, token_cols)], axis=0
        )

    pieces = [
        rows_of(tokens, tok_x),
        rows_of(tok_c[0], tok_c[1]),
        rows_of(tok_y, tok_xy),
        rows_of(tok_yc[0], tok_yc[1]),
    ]
    picks = jnp.arange(8, dtype=jnp.int32)
    swap_c, swap_x, swap_y = (picks >> 2) & 1, (picks >> 1) & 1, picks & 1
    row_order = swap_x * 4 + (tile ^ (swap_y * 2 + swap_c))
    order = jnp.concatenate([row_order, tile ^ jnp.arange(4, dtype=jnp.int32)]).astype(jnp.int32)
    normed, own_tokens = normalise(pieces, order, ln_gain)

    up_whole = jnp.zeros((width, half), BF)
    for k in range(layers):
        base = (layer ^ k) * block_cols
        up_whole = lax.dynamic_update_slice(up_whole, up_own_blocks[k], (base + side * depth, 0))
        up_whole = lax.dynamic_update_slice(
            up_whole, up_other_blocks[k], (base + (1 - side) * depth, 0)
        )
    pre = jnp.dot(normed, up_whole, preferred_element_type=F32)
    hidden = jax.nn.gelu(pre, approximate=True).astype(BF)

    count = hidden.shape[0]
    flux_pre = jnp.zeros((quarter, w_flux_in.shape[1]), F32)
    atm = jnp.zeros((quarter, width), BF)
    for k in range(layers):
        base = (layer ^ k) * block_cols
        terms = jnp.dot(hidden, down_blocks[k], preferred_element_type=F32).astype(BF)
        away = across_core(terms[count // 2 :])
        sums = (terms[: count // 2].astype(F32) + away.astype(F32)).astype(BF)
        away = across_x(sums[count // 4 :])
        sums = (sums[: count // 4].astype(F32) + away.astype(F32)).astype(BF)
        away = across_y(sums[count // 8 :])
        delta = sums[: count // 8].astype(F32) + away.astype(F32)
        mine = lax.dynamic_slice(own_tokens, (0, base), (quarter, block_cols))
        part = (mine.astype(F32) + delta).astype(BF)
        atm = lax.dynamic_update_slice(atm, part, (0, base))
        flux_rows = lax.dynamic_slice(flux_in, (base, 0), (block_cols, flux_in.shape[1]))
        flux_pre = flux_pre + jnp.dot(part, flux_rows, preferred_element_type=F32)

    flux_hidden = jax.nn.gelu(flux_pre, approximate=True).astype(BF)
    fluxes = jnp.dot(flux_hidden, w_flux_out, preferred_element_type=F32).astype(BF)

    bands = lax.axis_size("fsdp")
    edge = []
    for i in range(bands - 1):
        edge += [(4 * i + 3, 4 * i + 4), (4 * i + 4, 4 * i + 3)]
    rim = lax.ppermute(fluxes, ("fsdp", "tile"), edge)
    both = jnp.concatenate([fluxes, rim], axis=0)
    parts = [both, across_core(both), across_y(both), across_both(both)]
    window = jnp.zeros((6 * quarter, fluxes.shape[1]), BF)
    for i, piece in enumerate(parts):
        source = tile ^ i
        window = lax.dynamic_update_slice(window, piece[:quarter], ((1 + source) * quarter, 0))
    low_rim = sum(jnp.where((tile ^ i) == 0, parts[i][quarter:], 0) for i in range(4))
    high_rim = sum(jnp.where((tile ^ i) == 3, parts[i][quarter:], 0) for i in range(4))
    window = lax.dynamic_update_slice(window, low_rim, (0, 0))
    window = lax.dynamic_update_slice(window, high_rim, (5 * quarter, 0))

    grid_rows, wide_cols = wide_map.shape
    chans = ocean_state.shape[2]
    local_index = (wide_map - (band * band_rows - quarter)).reshape(-1)
    picked = jnp.take(window, jnp.clip(local_index, 0, window.shape[0] - 1), axis=0)
    forcing = jnp.dot(picked, w_couple, preferred_element_type=F32).reshape(
        grid_rows, wide_cols, chans
    )
    coupled = (
        wide_mask.astype(F32)[..., None] * (wide_state.astype(F32) + forcing)
    ).astype(BF)
    padded = side_halo(coupled, "fsdp", 0, halo)
    mask = full_mask.astype(F32)
    state = conv_block(
        padded, mask[3:-3, 3:-3], dw_kernel[0], ocean_gain[0], w_pw1[0], w_pw2[0]
    )
    state = conv_block(state, mask[6:-6, 6:-6], dw_kernel[1], ocean_gain[1], w_pw1[1], w_pw2[1])

    atm_out = jnp.zeros((band_rows, token_cols), BF)
    for i, shift in enumerate([None, across_core, across_y, across_both]):
        cols = lax.dynamic_slice(atm, (0, (tile ^ i) * token_cols), (quarter, token_cols))
        piece = cols if shift is None else shift(cols)
        atm_out = lax.dynamic_update_slice(atm_out, piece, ((tile ^ i) * quarter, 0))
    return (atm_out, state)


def solution(mesh):
    placed = (
        P("fsdp", "tile"),
        P(),
        P("fsdp", "tile"),
        P("tile", "fsdp"),
        P("tile", None),
        P(),
        P("fsdp", "tile", None),
        P("fsdp", "tile"),
        P("fsdp", "tile"),
        P(),
        P(),
        P(),
        P(),
        P(),
    )
    return jax.shard_map(
        body,
        mesh=mesh,
        in_specs=placed,
        out_specs=(P("fsdp", "tile"), P("fsdp", "tile", None)),
        check_vma=False,
    )
```

```python
import jax
import jax.numpy as jnp
from jax import lax
from jax.experimental import pallas as pl
from jax.experimental.pallas import tpu as pltpu
from jax.sharding import PartitionSpec as P

EPS = 1e-06
SLOPE = 0.7978845608028654
HALO = 6
PAD = 4
BF = jnp.bfloat16
F32 = jnp.float32
I32 = jnp.int32


def gelu(x):
    half = 0.5 * x
    return half + half * jnp.tanh(x * (SLOPE + SLOPE * 0.044715 * (x * x)))


def move(value, axis, target):
    count = lax.axis_size(axis)
    pairs = [(i, target(i)) for i in range(count)]
    return lax.ppermute(value, axis, [(i, j) for i, j in pairs if 0 <= j < count])


def across_x(value):
    return move(value, "fsdp", lambda i: i ^ 1)


def across_y(value):
    return move(value, "tile", lambda i: i ^ 2)


def across_core(value):
    return move(value, "tile", lambda i: i ^ 1)


def across_both(value):
    return move(value, "tile", lambda i: i ^ 3)


def next_pairs(i):
    return i + 1 if i % 2 else i - 1


def edge_swap(low, high, axis, even):
    near = move(jnp.where(even, high, low), axis, lambda i: i ^ 1)
    far = move(jnp.where(even, low, high), axis, next_pairs)
    return near, far


def line_move(value, pairs):
    both = [(2 * a + x, 2 * b + x) for a, b in pairs for x in range(2)]
    return lax.ppermute(value, "fsdp", both)


def line_gather(value):
    layers = lax.axis_size("fsdp") // 2
    if layers == 4:
        far = line_move(value, [(0, 2), (2, 0), (1, 3), (3, 1)])
        near = line_move(value, [(0, 1), (1, 0), (2, 3), (3, 2)])
        middle = line_move(value, [(1, 2), (2, 1)])
        outer = line_move(far, [(2, 3), (1, 0)])
        return [value, near, far, middle, outer]
    blocks = value[None]
    step = 1
    while step < layers:
        pairs = [(i, i ^ step) for i in range(layers)]
        blocks = jnp.concatenate([blocks, line_move(blocks, pairs)], axis=0)
        step *= 2
    return [blocks[i] for i in range(layers)]


def in_order(first, own, other, axis):
    return jnp.where(
        first,
        jnp.concatenate([own, other], axis=axis),
        jnp.concatenate([other, own], axis=axis),
    )


def norm_kernel(order, *refs):
    pieces = refs[:4]
    gain_ref, normed_ref, raw_ref = refs[4:]
    rows, width = pieces[0].shape[1:]
    whole = width * 4
    tall = rows // 4
    for j in range(4):
        at = pl.ds(j * tall, tall)
        values = [p[0, at, :].astype(F32) for p in pieces]
        mean = jnp.sum(sum(values), axis=-1, keepdims=True) / whole
        centers = [v - mean for v in values]
        spread = jnp.sum(sum(c * c for c in centers), axis=-1, keepdims=True) / whole
        scale = lax.rsqrt(spread + EPS)
        for i, center in enumerate(centers):
            start = pl.multiple_of(order[4 + i] * width, width)
            gain = gain_ref[:, pl.ds(start, width)]
            normed_ref[0, at, pl.ds(start, width)] = (center * scale * gain).astype(BF)

    @pl.when(pl.program_id(0) == 0)
    def _():
        for i, p in enumerate(pieces):
            start = pl.multiple_of(order[4 + i] * width, width)
            raw_ref[:, pl.ds(start, width)] = p[0]


def normalise(pieces, order, gain):
    rows = pieces[0].shape[0] // 4
    width = pieces[0].shape[1]
    whole = width * 4
    return pl.pallas_call(
        norm_kernel,
        out_shape=(
            jax.ShapeDtypeStruct((4, rows, whole), BF),
            jax.ShapeDtypeStruct((rows, whole), BF),
        ),
        grid_spec=pltpu.PrefetchScalarGridSpec(
            num_scalar_prefetch=1,
            grid=(4,),
            in_specs=[pl.BlockSpec((1, rows, width), lambda i, o: (o[i], 0, 0))] * 4
            + [pl.BlockSpec((1, whole), lambda i, o: (0, 0))],
            out_specs=(
                pl.BlockSpec((1, rows, whole), lambda i, o: (i, 0, 0)),
                pl.BlockSpec((rows, whole), lambda i, o: (0, 0)),
            ),
        ),
        name="normalise",
    )(order, *[p.reshape(4, rows, width) for p in pieces], gain.reshape(1, whole))


def up_kernel(order, own_ref, other_ref, *refs):
    blocks, out_ref, whole_ref = refs[:-2], refs[-2], refs[-1]
    step = pl.program_id(0)

    count = len(blocks)
    for k, block in enumerate(blocks):

        @pl.when((step == 0) & (order[count + k] != 0))
        def _(k=k, block=block):
            rows = block.shape[0]
            whole_ref[pl.ds(pl.multiple_of(order[k] * rows, rows), rows), :] = block[...]

    def run(ref):
        rows = ref.shape[0] * ref.shape[1]
        normed = ref[...].reshape(rows, ref.shape[2])
        pre = jnp.dot(normed, whole_ref[...], preferred_element_type=F32)
        out_ref[...] = gelu(pre).astype(BF)

    @pl.when(step % 2 == 0)
    def _():
        run(own_ref)

    @pl.when(step % 2 == 1)
    def _():
        run(other_ref)


def up_product(own, other, blocks, order):
    _, rows, whole = own.shape
    half = blocks[0].shape[1]
    return pl.pallas_call(
        up_kernel,
        out_shape=jax.ShapeDtypeStruct((8 * rows, half), BF),
        grid_spec=pltpu.PrefetchScalarGridSpec(
            num_scalar_prefetch=1,
            grid=(4,),
            in_specs=[
                pl.BlockSpec((2, rows, whole), lambda i, o: (i // 2, 0, 0)),
                pl.BlockSpec((2, rows, whole), lambda i, o: (i // 2, 0, 0)),
            ]
            + [pl.BlockSpec(b.shape, lambda i, o: (0, 0)) for b in blocks],
            out_specs=pl.BlockSpec((2 * rows, half), lambda i, o: (i, 0)),
            scratch_shapes=[pltpu.VMEM((whole, half), BF)],
        ),
        name="up_product",
    )(order, own, other, *blocks)


def head_kernel(order, *refs):
    count = (len(refs) - 12) // 2
    keeps, aways = refs[:count], refs[count : 2 * count]
    tokens_ref, w_out_ref = refs[2 * count : 2 * count + 2]
    flux_refs = refs[2 * count + 2 : 2 * count + 6]
    flux_out = refs[2 * count + 6]
    atm_refs = refs[2 * count + 7 : 2 * count + 11]
    atm = refs[2 * count + 11]
    cols = min(k.shape[1] for k in keeps)
    layers = tokens_ref.shape[1] // cols
    layer = 0
    for keep, away in zip(keeps, aways):
        for j in range(keep.shape[1] // cols):
            base = pl.multiple_of(order[layer] * cols, cols)
            here = pl.ds(j * cols, cols)
            delta = keep[:, here].astype(F32) + away[:, here].astype(F32)
            mine = tokens_ref[:, pl.ds(base, cols)].astype(F32)
            atm[:, pl.ds(base, cols)] = (mine + delta).astype(BF)
            layer += 1
    total = None
    for i in range(4):
        wide = flux_refs[i].shape[0]
        part = atm[:, pl.ds(pl.multiple_of(order[layers + i] * wide, wide), wide)]
        atm_refs[i][...] = part
        term = jnp.dot(part, flux_refs[i][...], preferred_element_type=F32)
        total = term if total is None else total + term
    flux_hidden = gelu(total).astype(BF)
    flux_out[...] = jnp.dot(flux_hidden, w_out_ref[...], preferred_element_type=F32).astype(BF)


def head(keeps, aways, own_tokens, w_flux_out, flux_pieces, order):
    rows, whole = own_tokens.shape
    return pl.pallas_call(
        head_kernel,
        out_shape=[jax.ShapeDtypeStruct((rows, w_flux_out.shape[1]), BF)]
        + [jax.ShapeDtypeStruct((rows, whole // 4), BF)] * 4,
        in_specs=[pl.BlockSpec(memory_space=pltpu.SMEM)]
        + [pl.BlockSpec(memory_space=pltpu.VMEM)] * (2 * len(keeps) + 6),
        out_specs=[pl.BlockSpec(memory_space=pltpu.VMEM)] * 5,
        scratch_shapes=[pltpu.VMEM((rows, whole), BF)],
        name="flux_head",
    )(order, *keeps, *aways, own_tokens, w_flux_out, *flux_pieces)


def couple_kernel(side, code_ref, state_ref, p0, p1, p2, p3, w_ref, out_ref, near_ref, far_ref):
    code = code_ref[...]
    rows = code.shape[0]
    span = p0.shape[0] // 2
    offset = code % span
    rest = code // span
    mask = (rest % 2).astype(F32)
    piece_of = rest // 2
    slots = lax.broadcasted_iota(I32, (rows, span), 1)
    hot = jnp.where(slots == offset, 1.0, 0.0).astype(BF)
    picked = None
    for i, piece in enumerate((p0, p1, p2, p3)):
        for j in range(2):
            term = jnp.dot(
                hot, piece[j * span : (j + 1) * span, :], preferred_element_type=F32
            )
            term = jnp.where(piece_of == 2 * i + j, term, 0.0)
            picked = term if picked is None else picked + term
    forcing = jnp.dot(picked.astype(BF), w_ref[...], preferred_element_type=F32)
    out_ref[...] = (mask * (state_ref[...].astype(F32) + forcing)).astype(BF)
    edge = near_ref.shape[0]
    step = pl.program_id(0)

    @pl.when((step == 0) & (side[0] == 0))
    def _():
        far_ref[...] = out_ref[:edge, :]

    @pl.when((step == 0) & (side[0] == 1))
    def _():
        near_ref[...] = out_ref[:edge, :]

    @pl.when((step == 1) & (side[0] == 0))
    def _():
        near_ref[...] = out_ref[rows - edge :, :]

    @pl.when((step == 1) & (side[0] == 1))
    def _():
        far_ref[...] = out_ref[rows - edge :, :]


def couple(side, code, state, pieces, w_couple, edge):
    rows, chans = state.shape
    tall = rows // 2
    tile_of = lambda cols: pl.BlockSpec((tall, cols), lambda i, o: (i, 0))
    fixed = lambda a: pl.BlockSpec(a.shape, lambda i, o: (0, 0))
    ends = pl.BlockSpec((edge, chans), lambda i, o: (0, 0))
    return pl.pallas_call(
        couple_kernel,
        out_shape=(
            jax.ShapeDtypeStruct((rows, chans), BF),
            jax.ShapeDtypeStruct((edge, chans), BF),
            jax.ShapeDtypeStruct((edge, chans), BF),
        ),
        grid_spec=pltpu.PrefetchScalarGridSpec(
            num_scalar_prefetch=1,
            grid=(2,),
            in_specs=[tile_of(1), tile_of(chans)]
            + [fixed(p) for p in pieces]
            + [fixed(w_couple)],
            out_specs=(tile_of(chans), ends, ends),
        ),
        name="couple",
    )(side.reshape(1).astype(I32), code, state, *pieces, w_couple)


def ocean_kernel(spots, *refs):
    mid, near, far, mask_a, mask_b, dw, gain, w_one, w_two = refs[:9]
    atm_pieces = refs[9:13]
    out_ref, atm_ref, wide, inner_state, normed = refs[13:]
    for i, piece in enumerate(atm_pieces):
        rows = piece.shape[0]
        atm_ref[pl.ds(pl.multiple_of(spots[2 + i] * rows, rows), rows), :] = piece[...]
    height = mid.shape[0]
    edge = near.shape[0]
    chans = mid.shape[2]
    span = wide.shape[2]

    def spread_row(ref, at, to):
        value = ref[at].astype(F32)
        for b in range(7):
            wide[b, to] = value[b : b + span, :]

    def spread_mid(i, carry):
        spread_row(mid, i, i + edge)
        return carry

    def spread_edge(i, carry):
        spread_row(near, i, spots[0] + i)
        spread_row(far, i, spots[1] + i)
        return carry

    lax.fori_loop(0, height, spread_mid, 0)
    lax.fori_loop(0, edge, spread_edge, 0)

    def block(k, source, rows, cols, mask_ref, store):
        lanes = 128
        parts = chans // lanes

        def conv(i, carry):
            row = 2 * i
            totals = []
            for h in range(parts):
                at = pl.ds(h * lanes, lanes)
                one = jnp.zeros((cols, lanes), F32)
                two = jnp.zeros((cols, lanes), F32)
                for a in range(8):
                    for b in range(7):
                        cell = source[b, row + a, :, at]
                        if a < 7:
                            one = one + cell * dw[pl.ds(k * 49 + a * 7 + b, 1), at]
                        if a > 0:
                            two = two + cell * dw[pl.ds(k * 49 + (a - 1) * 7 + b, 1), at]
                totals.append(jnp.concatenate([one, two], axis=0))
            mean = jnp.sum(sum(totals), axis=-1, keepdims=True) / chans
            centers = [t - mean for t in totals]
            spread = jnp.sum(sum(c * c for c in centers), axis=-1, keepdims=True) / chans
            scale = lax.rsqrt(spread + EPS)
            where = pl.ds(pl.multiple_of(2 * cols * i, 2 * cols), 2 * cols)
            for h in range(parts):
                at = pl.ds(h * lanes, lanes)
                normed[where, at] = (centers[h] * scale * gain[pl.ds(k, 1), at]).astype(BF)
            return carry

        lax.fori_loop(0, rows // 2, conv, 0)
        tall = rows // 2
        for part in range(2):
            first = part * tall
            pnorm = normed[first * cols : (first + tall) * cols, :]
            inner = jnp.dot(pnorm, w_one[k], preferred_element_type=F32)
            inner = gelu(inner).astype(BF)
            lowered = jnp.dot(inner, w_two[k], preferred_element_type=F32)
            lowered = lowered.reshape(tall, cols, chans)
            before = source[3, first + 3 : first + 3 + tall]
            store(first, tall, mask_ref[first : first + tall] * (before + lowered))

    def keep(first, tall, value):
        value = value.astype(BF).astype(F32)
        for b in range(7):
            inner_state[b, first : first + tall] = value[:, b : b + out_ref.shape[1], :]

    def give(first, tall, value):
        out_ref[first : first + tall] = value.astype(BF)

    block(0, wide, mask_a.shape[0], mask_a.shape[1], mask_a, keep)
    block(1, inner_state, mask_b.shape[0], mask_b.shape[1], mask_b, give)


def ocean(spots, mid, near, far, mask_a, mask_b, dw, gain, w_one, w_two, atm_pieces):
    height, _, chans = mid.shape
    rows, cols = mask_b.shape[:2]
    quarter, token_cols = atm_pieces[0].shape
    vmem = pl.BlockSpec(memory_space=pltpu.VMEM)
    return pl.pallas_call(
        ocean_kernel,
        out_shape=(
            jax.ShapeDtypeStruct((rows, cols, chans), BF),
            jax.ShapeDtypeStruct((4 * quarter, token_cols), BF),
        ),
        in_specs=[pl.BlockSpec(memory_space=pltpu.SMEM)] + [vmem] * 13,
        out_specs=(vmem, vmem),
        scratch_shapes=[
            pltpu.VMEM((7, height + 2 * HALO, mask_a.shape[1], chans), F32),
            pltpu.VMEM((7, mask_a.shape[0], cols, chans), F32),
            pltpu.VMEM((mask_a.shape[0] * mask_a.shape[1], chans), BF),
        ],
        name="ocean",
    )(spots, mid, near, far, mask_a, mask_b, dw, gain, w_one, w_two, *atm_pieces)


def body(
    tokens,
    ln_gain,
    w_up,
    w_down,
    w_flux_in,
    w_flux_out,
    ocean_state,
    land_mask,
    column_map,
    w_couple,
    dw_kernel,
    ocean_gain,
    w_pw1,
    w_pw2,
):
    band = lax.axis_index("fsdp")
    tile = lax.axis_index("tile")
    side = band % 2
    layer = band // 2
    first = side == 0
    layers = lax.axis_size("fsdp") // 2
    band_rows, token_cols = tokens.shape
    depth, hidden_cols = w_up.shape
    half = hidden_cols // 2
    quarter = band_rows // 4
    width = token_cols * 4
    block_cols = 2 * depth
    four = jnp.arange(4, dtype=I32)

    up_own = lax.dynamic_slice(w_up, (0, side * half), (depth, half))
    up_away = lax.dynamic_slice(w_up, (0, (1 - side) * half), (depth, half))
    up_other = across_x(up_away)
    up_blocks = line_gather(up_own) + line_gather(up_other)

    tok_x = across_x(tokens)
    tok_y = across_y(tokens)
    tok_xy = jnp.concatenate(
        [across_y(tok_x[: band_rows // 2]), across_x(tok_y[band_rows // 2 :])],
        axis=0,
    )
    own = [tokens, across_core(tokens), tok_y, across_core(tok_y)]
    other = [tok_x, across_core(tok_x), tok_xy, across_core(tok_xy)]

    down_own = lax.dynamic_slice(w_down, (side * half, 0), (half, depth))
    down_away = lax.dynamic_slice(w_down, ((1 - side) * half, 0), (half, depth))
    down_other = across_x(down_away)
    down_blocks = line_gather(in_order(first, down_own, down_other, 1))
    inner = (layer == 1) | (layer == 2)
    if layers == 4:
        down_blocks = down_blocks[:3] + [jnp.where(inner, down_blocks[3], down_blocks[4])]

    flux_y = across_y(w_flux_in)
    flux_pieces = [w_flux_in, across_core(w_flux_in), flux_y, across_core(flux_y)]

    grid_rows, grid_cols, chans = ocean_state.shape
    even = tile % 2 == 0

    def widen(value, axis):
        low_edge = lax.slice_in_dim(value, 0, HALO, axis=axis)
        high_edge = lax.slice_in_dim(value, grid_cols - HALO, None, axis=axis)
        near, far = edge_swap(low_edge, high_edge, "tile", even)
        low = jnp.where(even, far, near)
        high = jnp.where(even, near, far)
        blank = jnp.zeros(value.shape[:axis] + (PAD,) + value.shape[axis + 1 :], value.dtype)
        return jnp.concatenate([low, value, high, blank], axis=axis)

    ints = widen(jnp.stack([column_map, land_mask]), 2)
    wide_state = widen(ocean_state, 1)
    wide_map, wide_mask = ints[0], ints[1]
    near, far = edge_swap(wide_mask[:HALO], wide_mask[-HALO:], "fsdp", first)
    full_mask = jnp.concatenate(
        [jnp.where(first, far, near), wide_mask, jnp.where(first, near, far)], axis=0
    ).astype(F32)
    ring = HALO // 2
    out_cols = grid_cols + HALO
    pad_cols = -(-out_cols // 8) * 8
    mask_a = jnp.pad(
        full_mask[ring : ring + grid_rows + HALO, ring : ring + out_cols],
        ((0, 0), (0, pad_cols - out_cols)),
    )[..., None]
    mask_b = land_mask.astype(F32)[..., None]

    local = jnp.clip(wide_map - (band * band_rows - quarter), 0, 6 * quarter - 1)
    source = jnp.clip(local // quarter - 1, 0, 3)
    offset = local - (source + 1) * quarter
    beyond = (offset < 0) | (offset >= quarter)
    offset = jnp.where(offset < 0, offset + quarter, jnp.where(beyond, offset - quarter, offset))
    piece_of = (source ^ tile) * 2 + beyond.astype(I32)
    span = wide_map.shape[1]

    order = jnp.concatenate([tile ^ (four % 2 * 2 + four // 2), tile ^ four])
    normed_own, own_tokens = normalise(own, order, ln_gain)
    normed_other, _ = normalise(other, order, ln_gain)
    layer_order = layer ^ jnp.arange(layers, dtype=I32)
    head_order = jnp.concatenate([layer_order, tile ^ four])
    if layers == 4:
        slot = layer ^ jnp.array([0, 1, 2, 3, 3], I32)
        outside = 1 - inner.astype(I32)
        live = jnp.stack([outside | 1] * 3 + [1 - outside, outside])
    else:
        slot = layer_order
        live = jnp.ones((layers,), I32)
    up_order = jnp.concatenate([slot * 2 + side, slot * 2 + 1 - side, live, live])
    end = grid_rows + HALO
    spots = jnp.concatenate(
        [jnp.stack([jnp.where(first, end, 0), jnp.where(first, 0, end)]), tile ^ four]
    ).astype(I32)
    code = ((piece_of * 2 + wide_mask) * quarter + offset).reshape(-1, 1)
    flat_state = wide_state.reshape(-1, chans)
    taps = dw_kernel.reshape(-1, chans)
    normed_other, up_order, head_order, spots, code, flat_state, taps, mask_a, mask_b = (
        lax.optimization_barrier(
            (normed_other, up_order, head_order, spots, code, flat_state, taps, mask_a, mask_b)
        )
    )
    hidden = up_product(normed_own, normed_other, up_blocks, up_order)

    count = hidden.shape[0]
    keeps, aways = [], []
    groups = [jnp.concatenate(down_blocks[:2], axis=1)] + down_blocks[2:]
    for group in groups:
        terms = jnp.dot(hidden, group, preferred_element_type=F32).astype(BF)
        away = across_core(terms[count // 2 :])
        sums = (terms[: count // 2].astype(F32) + away.astype(F32)).astype(BF)
        away = across_x(sums[count // 4 :])
        sums = (sums[: count // 4].astype(F32) + away.astype(F32)).astype(BF)
        keeps.append(sums[: count // 8])
        aways.append(across_y(sums[count // 8 :]))

    if block_cols % 128 == 0:
        fluxes, *atm = head(
            keeps,
            aways,
            own_tokens,
            w_flux_out,
            flux_pieces,
            head_order,
        )
    else:
        whole = jnp.zeros((quarter, width), F32)
        delta = jnp.concatenate(keeps, axis=1).astype(F32)
        delta = delta + jnp.concatenate(aways, axis=1).astype(F32)
        for k in range(layers):
            piece = delta[:, k * block_cols : (k + 1) * block_cols]
            whole = lax.dynamic_update_slice(whole, piece, (0, (layer ^ k) * block_cols))
        whole = (own_tokens.astype(F32) + whole).astype(BF)
        atm = [
            lax.dynamic_slice(whole, (0, (tile ^ i) * token_cols), (quarter, token_cols))
            for i in range(4)
        ]
        flux_pre = sum(
            jnp.dot(a, w, preferred_element_type=F32) for a, w in zip(atm, flux_pieces)
        )
        flux_hidden = gelu(flux_pre).astype(BF)
        fluxes = jnp.dot(flux_hidden, w_flux_out, preferred_element_type=F32).astype(BF)

    bands = lax.axis_size("fsdp")
    ends = []
    for i in range(bands - 1):
        ends += [(4 * i + 3, 4 * i + 4), (4 * i + 4, 4 * i + 3)]
    rim = lax.ppermute(fluxes, ("fsdp", "tile"), ends)
    both = jnp.concatenate([fluxes, rim], axis=0)
    pieces = [both, across_core(both), across_y(both), across_both(both)]
    coupled, near, far = couple(side, code, flat_state, pieces, w_couple, HALO * span)
    near = move(near.reshape(HALO, span, chans), "fsdp", lambda i: i ^ 1)
    far = move(far.reshape(HALO, span, chans), "fsdp", next_pairs)
    coupled = coupled.reshape(grid_rows, span, chans)

    atm_pieces = [atm[0], across_core(atm[1]), across_y(atm[2]), across_both(atm[3])]
    state, atm_out = ocean(
        spots,
        coupled,
        near,
        far,
        mask_a,
        mask_b,
        taps,
        ocean_gain,
        w_pw1,
        w_pw2,
        atm_pieces,
    )
    return (atm_out, state)


def solution(mesh):
    placed = (
        P("fsdp", "tile"),
        P(),
        P("fsdp", "tile"),
        P("tile", "fsdp"),
        P("tile", None),
        P(),
        P("fsdp", "tile", None),
        P("fsdp", "tile"),
        P("fsdp", "tile"),
        P(),
        P(),
        P(),
        P(),
        P(),
    )
    return jax.shard_map(
        body,
        mesh=mesh,
        in_specs=placed,
        out_specs=(P("fsdp", "tile"), P("fsdp", "tile", None)),
        check_vma=False,
    )
```
